32 devices in a mesh: samp: 16 (over z, x, core), snp: 2 (over y).
Axes of the slice: x: 2, y: 2, z: 4, core: 2. Of those that a mesh axis runs over, the one named last changes fastest.
Arguments:
- genotypes: int32 [65536, 4096], P('samp', 'snp'), may hold values from 0 to 2, as said below
- allele_freq: float32 [4096], P('snp'), may hold values from 0.05 to 0.5
- snp_bins: int32 [4096], P('snp'), may hold values from 0 to 11, as said below
- probes: bfloat16 [64, 65536], P(None, 'samp'), may hold values from -6 to 6
- variances: float32 [13], replicated, may hold values from 0.1 to 1
Outputs:
- projected: float32 [65536, 768], P(('samp', 'snp'))
- combined: float32 [64, 65536], P(None, ('samp', 'snp'))
The draws below stay inside these ranges and needn't reach their ends.
Inputs may be any that keep to these rules, and one draw needn't show every extreme that they name: `genotypes`: dosages 0, 1 or 2. `snp_bins`: every component has at least one SNP.
All inputs are finite; a program needn't handle non-finite values.
Results may differ from the reference program's by a relative error of at most 0.0065.
Values may be sent and summed in bfloat16 or wider, within the bound.
A program may use at most 192 MiB of HBM per device.

```python
import math
import jax
import jax.numpy as jnp
from jax import lax

SNPS = 4096
COMPONENTS = 12
PROBES = 64
ROWS = 4096
SAMPLES = 65536
N_SAMP = 16


def allele_draw(key):
    seeded = jax.random.fold_in(key, 7)
    allele_level = jax.random.randint(jax.random.fold_in(seeded, 1), (SNPS,), 50, 501, dtype=jnp.int32)
    first_copy = jax.random.randint(jax.random.fold_in(seeded, 2), (SAMPLES, SNPS), 0, 1000, dtype=jnp.int32)
    second_copy = jax.random.randint(jax.random.fold_in(seeded, 3), (SAMPLES, SNPS), 0, 1000, dtype=jnp.int32)
    dosage = (first_copy < allele_level[None, :]).astype(jnp.int32) + (second_copy < allele_level[None, :]).astype(jnp.int32)
    return (dosage, allele_level.astype(jnp.float32) / 1000.0)


def draw_genotypes(key, part):
    return allele_draw(key)[0]


def draw_allele_freq(key, part):
    return allele_draw(key)[1]


def draw_snp_bins(key, part):
    seeded = jax.random.fold_in(key, 11)
    places = jax.random.permutation(jax.random.fold_in(seeded, 1), SNPS).astype(jnp.int32)
    first_level = jax.random.randint(jax.random.fold_in(seeded, 2), (SNPS,), 0, COMPONENTS, dtype=jnp.int32)
    second_level = jax.random.randint(jax.random.fold_in(seeded, 3), (SNPS,), 0, COMPONENTS, dtype=jnp.int32)
    skewed = first_level * second_level // (COMPONENTS - 1)
    base_bins = jnp.where(places < COMPONENTS, places, skewed).astype(jnp.int32)
    relabel = jax.random.permutation(jax.random.fold_in(seeded, 4), COMPONENTS).astype(jnp.int32)
    return relabel[base_bins].astype(jnp.int32)


def block_scale(own_key, dims, shards, low, largest):
    def one(position, parts):
        draws = jax.random.uniform(jax.random.fold_in(jax.random.fold_in(own_key, 6), position), (parts,), jnp.float32, low / len(shards), largest / len(shards))
        return jnp.repeat(jnp.exp(draws), dims[position] // parts).reshape((-1,) + (1,) * (len(dims) - position - 1))

    gain = one(*shards[0])
    for cut in shards[1:]:
        gain = gain * one(*cut)
    return gain


def noise(key, dims, scale, limit, shards=(), kind=jnp.bfloat16):
    factor_of = block_scale(key, dims, shards, -0.22, 0.18) if shards else 1.0
    drawn = jax.random.normal(key, dims, jnp.float32) * scale * factor_of
    return jnp.minimum(jnp.maximum(drawn, -limit), limit).astype(kind)


def setup_inputs(seed: int = 0) -> dict:
    keys = jax.random.split(jax.random.key(seed), 6)
    return {
        "genotypes": draw_genotypes(jax.random.fold_in(keys[5], 71), 0),
        "allele_freq": draw_allele_freq(jax.random.fold_in(keys[5], 71), 0),
        "snp_bins": draw_snp_bins(jax.random.fold_in(keys[5], 71), 0),
        "probes": noise(keys[3], (PROBES, SAMPLES), 1.0, 6.0, ((1, 16),)),
        "variances": jnp.clip(jnp.exp(jax.random.uniform(keys[4], (COMPONENTS + 1,), jnp.float32, math.log(0.1), math.log(1.0))), 0.1, 1.0),
    }


def standardize(dosage_block, allele_freq):
    spread = jnp.sqrt(2.0 * allele_freq * (1.0 - allele_freq))
    return ((dosage_block.astype(jnp.float32) - 2.0 * allele_freq) / spread).astype(jnp.bfloat16)

def reference(genotypes, allele_freq, snp_bins, probes, variances):
    dosage_blocks = genotypes.reshape(N_SAMP, ROWS, SNPS)
    probe_blocks = probes.reshape(PROBES, N_SAMP, ROWS).transpose(1, 0, 2)

    def accumulate(carry, pieces):
        dosage_block, probe_block = pieces
        standard = standardize(dosage_block, allele_freq)
        return (carry + jnp.dot(probe_block, standard, preferred_element_type=jnp.float32), None)
    scores, _ = lax.scan(accumulate, jnp.zeros((PROBES, SNPS), jnp.float32), (dosage_blocks, probe_blocks))
    scores = scores / jnp.sqrt(jnp.float32(SAMPLES))
    labels = jnp.arange(COMPONENTS, dtype=jnp.int32)
    onehot = (snp_bins[:, None] == labels[None, :]).astype(jnp.float32)
    counts = lax.optimization_barrier(jnp.sum(onehot, 0))
    factor = lax.optimization_barrier(jnp.sum(onehot * lax.rsqrt(counts)[None, :], 1))
    weights = ((scores.T * factor[:, None])[:, None, :] * onehot[:, :, None]).reshape(SNPS, COMPONENTS * PROBES).astype(jnp.bfloat16)

    def project(dosage_block):
        return jnp.dot(standardize(dosage_block, allele_freq), weights, preferred_element_type=jnp.float32)
    projected = lax.map(project, dosage_blocks).reshape(SAMPLES, COMPONENTS * PROBES)
    stacked = projected.reshape(SAMPLES, COMPONENTS, PROBES)
    combined = jnp.einsum('nmb,m->bn', stacked, variances[:COMPONENTS]) + variances[COMPONENTS] * probes.astype(jnp.float32)
    return (projected, combined)
```

```python
import jax
import jax.numpy as jnp
from jax import lax
from jax.sharding import PartitionSpec as P

COMPONENTS = 12
CHUNKS = 4


def standardize(dosage_block, allele_freq):
    spread = jnp.sqrt(2.0 * allele_freq * (1.0 - allele_freq))
    return ((dosage_block.astype(jnp.float32) - 2.0 * allele_freq) / spread).astype(jnp.bfloat16)


def body(genotypes, allele_freq, snp_bins, probes, variances):
    groups = lax.axis_size("snp")
    me = lax.axis_index("snp")
    labels = jnp.arange(COMPONENTS, dtype=jnp.int32)
    onehot = (snp_bins[:, None] == labels[None, :]).astype(jnp.float32)
    counts = lax.psum(jnp.sum(onehot, 0), "snp")
    standard = standardize(genotypes, allele_freq)
    partial_scores = jnp.dot(probes, standard, preferred_element_type=jnp.float32)
    whole_rows = standard.shape[0] * lax.axis_size("samp")
    scores = lax.psum(partial_scores, "samp") / jnp.sqrt(jnp.float32(whole_rows))
    factor = jnp.sum(onehot * lax.rsqrt(counts)[None, :], 1)
    width = scores.shape[0]
    weights = ((scores.T * factor[:, None])[:, None, :] * onehot[:, :, None]).reshape(
        snp_bins.shape[0], COMPONENTS * width
    ).astype(jnp.bfloat16)
    own_rows = standard.shape[0] // groups
    piece = own_rows // CHUNKS

    def product(target, chunk):
        rows = lax.dynamic_slice_in_dim(standard, target * own_rows + chunk * piece, piece, 0)
        return jnp.dot(rows, weights, preferred_element_type=jnp.float32)

    got = [[] for _ in range(CHUNKS)]
    for shift in range(1, groups):
        ring = [(i, (i + shift) % groups) for i in range(groups)]
        for chunk in range(CHUNKS):
            sent = product(lax.rem(me + shift, groups), chunk).astype(jnp.bfloat16)
            got[chunk].append(lax.ppermute(sent, "snp", ring))
    blocks = []
    for chunk in range(CHUNKS):
        total = product(me, chunk)
        for term in got[chunk]:
            total = total + term.astype(jnp.float32)
        blocks.append(total)
    projected = jnp.concatenate(blocks, 0)
    stacked = projected.reshape(own_rows, COMPONENTS, width)
    own_probes = lax.dynamic_slice_in_dim(probes, me * own_rows, own_rows, 1).astype(jnp.float32)
    combined = (
        jnp.einsum("nmb,m->bn", stacked, variances[:COMPONENTS])
        + variances[COMPONENTS] * own_probes
    )
    return (projected, combined)


def solution(mesh):
    placed = (P("samp", "snp"), P("snp"), P("snp"), P(None, "samp"), P())
    return jax.shard_map(
        body,
        mesh=mesh,
        in_specs=placed,
        out_specs=(P(("samp", "snp"), None), P(None, ("samp", "snp"))),
        check_vma=False,
    )
```

```python
import functools

import jax
import jax.numpy as jnp
from jax import lax
from jax.experimental import pallas as pl
from jax.experimental.pallas import tpu as pltpu
from jax.sharding import PartitionSpec as P

COMPONENTS = 12
LABELS = 16
LANES = 128
TILE_BYTES = 2 << 20
DEPTH = 3
MESH = pl.DeviceIdType.MESH
F32 = jnp.float32
BF16 = jnp.bfloat16


class Plan:
    def __init__(self, rows, snps, width, samp, snp):
        self.rows, self.snps, self.width = rows, snps, width
        self.samp, self.snp = samp, snp
        self.total = COMPONENTS * width
        self.parts = 1
        for parts in (2,):
            span = snps // parts
            if span % LANES == 0 and width // (samp // min(samp, span // LANES)) >= 16:
                self.parts = parts
        self.span = snps // self.parts
        self.across = min(samp, self.span // LANES)
        self.down = samp // self.across
        self.high = width // self.down
        self.wide = self.span // self.across
        self.tile = min(rows, TILE_BYTES // (4 * self.span))
        self.tiles = rows // self.tile
        self.own = rows // snp
        self.chunk = min(256, self.own)
        self.chunks = self.own // self.chunk


def kernel(
    plan, geno, freq, bins, probes, lane_vars, noise_var, out, comb,
    dosages, standard, acc, rs_send, rs_recv, gathered, counts, factor, weights,
    part_send, part_recv, own, comb_rows,
    in_sem, rs_ssem, rs_rsem, ag_ssem, ag_rsem, ct_ssem, ct_rsem, ex_ssem, ex_rsem, out_sem, comb_sem,
):
    p = plan
    n, groups = p.samp, p.snp
    me, mine = lax.axis_index("samp"), lax.axis_index("snp")

    def fetch(step):
        part, tile, slot = step // p.tiles, step % p.tiles, step % DEPTH
        return pltpu.make_async_copy(
            geno.at[pl.ds(tile * p.tile, p.tile), pl.ds(pl.multiple_of(part * p.span, LANES), p.span)],
            dosages.at[slot],
            in_sem.at[slot],
        )

    steps = p.parts * p.tiles
    for step in range(min(DEPTH - 1, steps)):
        fetch(step).start()

    barrier = pltpu.get_barrier_semaphore()

    @pl.loop(1, n)
    def _(shift):
        pl.semaphore_signal(
            barrier, inc=1, device_id={"samp": (me + shift) % n, "snp": mine}, device_id_type=MESH
        )

    @pl.loop(1, groups)
    def _(shift):
        pl.semaphore_signal(
            barrier, inc=1, device_id={"samp": me, "snp": (mine + shift) % groups}, device_id_type=MESH
        )

    labels = lax.broadcasted_iota(jnp.int32, (LABELS, p.snps), 0)
    hits = labels == bins[...]
    counted = jnp.sum(hits.astype(F32), axis=1, keepdims=True)
    counts[0] = jnp.broadcast_to(counted, (LABELS, LANES))
    acc[...] = jnp.zeros_like(acc)
    pl.semaphore_wait(barrier, n - 1 + groups - 1)

    def count_copy(shift):
        return pltpu.make_async_remote_copy(
            src_ref=counts.at[0], dst_ref=counts.at[shift],
            send_sem=ct_ssem.at[shift - 1], recv_sem=ct_rsem.at[shift - 1],
            device_id={"samp": me, "snp": (mine + shift) % groups}, device_id_type=MESH,
        )

    for shift in range(1, groups):
        count_copy(shift).start()

    def scatter_copy(part, shift):
        peer = (me + shift) % n
        return pltpu.make_async_remote_copy(
            src_ref=rs_send.at[part, peer], dst_ref=rs_recv.at[part, shift - 1],
            send_sem=rs_ssem.at[part, shift - 1], recv_sem=rs_rsem.at[part, shift - 1],
            device_id={"samp": peer, "snp": mine}, device_id_type=MESH,
        )

    def gather_copy(part, shift):
        return pltpu.make_async_remote_copy(
            src_ref=gathered.at[part, me], dst_ref=gathered.at[part, me],
            send_sem=ag_ssem.at[part, shift - 1], recv_sem=ag_rsem.at[part, shift - 1],
            device_id={"samp": (me + shift) % n, "snp": mine}, device_id_type=MESH,
        )

    def arrival(part, shift):
        source = (me + n - shift) % n
        return pltpu.make_async_remote_copy(
            src_ref=gathered.at[part, source], dst_ref=gathered.at[part, source],
            send_sem=ag_ssem.at[part, shift - 1], recv_sem=ag_rsem.at[part, shift - 1],
            device_id={"samp": source, "snp": mine}, device_id_type=MESH,
        )

    def read_part(part):
        columns = slice(part * p.span, (part + 1) * p.span)
        allele = freq[:, columns]
        center = 2.0 * allele
        scale = 1.0 / jnp.sqrt(center * (1.0 - allele))

        @pl.loop(0, p.tiles)
        def _(tile):
            step = part * p.tiles + tile

            @pl.when(step + DEPTH - 1 < steps)
            def _():
                fetch(step + DEPTH - 1).start()

            fetch(step).wait()
            rows = pl.ds(pl.multiple_of(tile * p.tile, p.tile), p.tile)
            value = ((dosages[step % DEPTH].astype(F32) - center) * scale).astype(BF16)
            standard[rows, columns] = value
            acc[:, columns] += jnp.dot(probes[:, rows], value, preferred_element_type=F32)

        for piece in range(n):
            top, left = (piece // p.across) * p.high, part * p.span + (piece % p.across) * p.wide
            rs_send[part, piece] = acc[top : top + p.high, left : left + p.wide].astype(BF16)

        @pl.loop(1, n)
        def _(shift):
            scatter_copy(part, shift).start()

    def reduce_part(part):
        def add(shift, total):
            scatter_copy(part, shift).wait_recv()
            return total + rs_recv[part, shift - 1].astype(F32)

        total = lax.fori_loop(1, n, add, rs_send[part, me].astype(F32))
        left = pl.multiple_of(part * p.span + (me % p.across) * p.wide, LANES)
        whole_rows = jnp.float32(p.rows * n)
        scores = total / jnp.sqrt(whole_rows)
        gathered[part, me] = (scores * factor[0:1, pl.ds(left, p.wide)]).astype(BF16)

        @pl.loop(1, n)
        def _(shift):
            gather_copy(part, shift).start()

    def spread_part(part):
        @pl.loop(1, n)
        def _(shift):
            arrival(part, shift).wait_recv()

        repeat = LANES // p.width
        for column in range(p.across):
            left = part * p.span + column * p.wide
            pieces = [gathered[part, column + p.across * row].astype(F32) for row in range(p.down)]
            block = jnp.concatenate(pieces * repeat, axis=0)
            turned = block.T
            marks = jnp.broadcast_to(bins[:, left : left + p.wide].astype(F32), (LANES, p.wide)).T
            lane = lax.broadcasted_iota(jnp.int32, (p.wide, LANES), 1) // p.width
            for pair in range(p.total // LANES):
                label = (lane + pair * repeat).astype(F32)
                weights[left : left + p.wide, pair * LANES : (pair + 1) * LANES] = jnp.where(
                    marks == label, turned, 0.0
                ).astype(BF16)

    read_part(0)
    for shift in range(1, groups):
        count_copy(shift).wait_recv()
    whole = counts[0]
    for shift in range(1, groups):
        whole = whole + counts[shift]
    root = lax.rsqrt(whole[:, 0:1])
    row = jnp.sum(jnp.where(hits, root, 0.0), axis=0, keepdims=True)
    factor[...] = jnp.broadcast_to(row, factor.shape)
    for part in range(1, p.parts):
        read_part(part)
        reduce_part(part - 1)
    reduce_part(p.parts - 1)
    for part in range(p.parts):
        spread_part(part)

    def part_copy(index):
        shift, chunk = index // p.chunks, index % p.chunks
        rows = pl.ds(pl.multiple_of(chunk * p.chunk, p.chunk), p.chunk)
        return pltpu.make_async_remote_copy(
            src_ref=part_send.at[shift, rows], dst_ref=part_recv.at[shift, rows],
            send_sem=ex_ssem.at[index], recv_sem=ex_rsem.at[index],
            device_id={"samp": me, "snp": (mine + shift + 1) % groups}, device_id_type=MESH,
        )

    sends = (groups - 1) * p.chunks

    @pl.loop(0, sends)
    def _(index):
        shift, chunk = index // p.chunks, index % p.chunks
        target = (mine + shift + 1) % groups
        rows = pl.ds(pl.multiple_of(target * p.own + chunk * p.chunk, p.chunk), p.chunk)
        product = jnp.dot(standard[rows, :], weights[...], preferred_element_type=F32)
        part_send[shift, pl.ds(pl.multiple_of(chunk * p.chunk, p.chunk), p.chunk), :] = product.astype(BF16)
        part_copy(index).start()

    @pl.loop(0, p.chunks)
    def _(chunk):
        rows = pl.ds(pl.multiple_of(mine * p.own + chunk * p.chunk, p.chunk), p.chunk)
        here = pl.ds(pl.multiple_of(chunk * p.chunk, p.chunk), p.chunk)
        own[here, :] = jnp.dot(standard[rows, :], weights[...], preferred_element_type=F32)

    def out_copy(chunk):
        here = pl.ds(pl.multiple_of(chunk * p.chunk, p.chunk), p.chunk)
        return pltpu.make_async_copy(own.at[here], out.at[here], out_sem.at[chunk])

    def comb_copy(chunk):
        here = pl.ds(pl.multiple_of(chunk * p.chunk, p.chunk), p.chunk)
        return pltpu.make_async_copy(comb_rows.at[chunk], comb.at[:, here], comb_sem.at[chunk])

    @pl.loop(0, p.chunks)
    def _(chunk):
        here = pl.ds(pl.multiple_of(chunk * p.chunk, p.chunk), p.chunk)
        total = own[here, :]
        for shift in range(groups - 1):
            part_copy(shift * p.chunks + chunk).wait_recv()
            total = total + part_recv[shift, here, :].astype(F32)
        own[here, :] = total
        out_copy(chunk).start()
        folded = jnp.zeros((p.chunk, LANES), F32)
        for pair in range(p.total // LANES):
            lanes = slice(pair * LANES, (pair + 1) * LANES)
            folded = folded + total[:, lanes] * lane_vars[:, lanes]
        turned = folded.T
        mixed = turned[0 : p.width]
        for again in range(1, LANES // p.width):
            mixed = mixed + turned[again * p.width : (again + 1) * p.width]
        cols = pl.ds(pl.multiple_of(mine * p.own + chunk * p.chunk, p.chunk), p.chunk)
        comb_rows[chunk] = mixed + noise_var[:, 0:1] * probes[:, cols].astype(F32)
        comb_copy(chunk).start()

    @pl.loop(0, sends)
    def _(index):
        part_copy(index).wait_send()

    for part in range(p.parts):

        @pl.loop(1, n)
        def _(shift):
            scatter_copy(part, shift).wait_send()
            gather_copy(part, shift).wait_send()

    for shift in range(1, groups):
        count_copy(shift).wait_send()

    @pl.loop(0, p.chunks)
    def _(chunk):
        out_copy(chunk).wait()
        comb_copy(chunk).wait()


def body(genotypes, allele_freq, snp_bins, probes, variances):
    rows, snps = genotypes.shape
    width = probes.shape[0]
    p = Plan(rows, snps, width, lax.axis_size("samp"), lax.axis_size("snp"))
    n, groups = p.samp, p.snp
    lane_vars = jnp.repeat(variances[:COMPONENTS], width)[None, :]
    noise_var = jnp.broadcast_to(variances[COMPONENTS], (1, LANES))
    vmem, hbm = pl.BlockSpec(memory_space=pltpu.VMEM), pl.BlockSpec(memory_space=pl.ANY)
    dma = pltpu.SemaphoreType.DMA
    sends = (groups - 1) * p.chunks
    return pl.pallas_call(
        functools.partial(kernel, p),
        out_shape=(
            jax.ShapeDtypeStruct((p.own, p.total), F32),
            jax.ShapeDtypeStruct((width, p.own), F32),
        ),
        in_specs=[hbm, vmem, vmem, vmem, vmem, vmem],
        out_specs=(hbm, hbm),
        scratch_shapes=[
            pltpu.VMEM((DEPTH, p.tile, p.span), jnp.int32),
            pltpu.VMEM((rows, snps), BF16),
            pltpu.VMEM((width, snps), F32),
            pltpu.VMEM((p.parts, n, p.high, p.wide), BF16),
            pltpu.VMEM((p.parts, n - 1, p.high, p.wide), BF16),
            pltpu.VMEM((p.parts, n, p.high, p.wide), BF16),
            pltpu.VMEM((groups, LABELS, LANES), F32),
            pltpu.VMEM((8, snps), F32),
            pltpu.VMEM((snps, p.total), BF16),
            pltpu.VMEM((groups - 1, p.own, p.total), BF16),
            pltpu.VMEM((groups - 1, p.own, p.total), BF16),
            pltpu.VMEM((p.own, p.total), F32),
            pltpu.VMEM((p.chunks, width, p.chunk), F32),
            dma((DEPTH,)),
            dma((p.parts, n - 1)), dma((p.parts, n - 1)),
            dma((p.parts, n - 1)), dma((p.parts, n - 1)),
            dma((groups - 1,)), dma((groups - 1,)),
            dma((sends,)), dma((sends,)),
            dma((p.chunks,)), dma((p.chunks,)),
        ],
        compiler_params=pltpu.CompilerParams(
            collective_id=0, has_side_effects=True, vmem_limit_bytes=60 << 20
        ),
    )(genotypes, allele_freq[None, :], snp_bins[None, :], probes, lane_vars, noise_var)


def solution(mesh):
    placed = (P("samp", "snp"), P("snp"), P("snp"), P(None, "samp"), P())
    return jax.shard_map(
        body,
        mesh=mesh,
        in_specs=placed,
        out_specs=(P(("samp", "snp"), None), P(None, ("samp", "snp"))),
        check_vma=False,
    )
```

```python
import functools

import jax
import jax.numpy as jnp
from jax import lax
from jax.experimental import pallas as pl
from jax.experimental.pallas import tpu as pltpu
from jax.sharding import PartitionSpec as P

COMPONENTS = 12
LABELS = 16
LANES = 128
TILE_BYTES = 2 << 20
DEPTH = 3
MESH = pl.DeviceIdType.MESH
F32 = jnp.float32
BF16 = jnp.bfloat16


class Plan:
    def __init__(self, rows, snps, width, samp, snp):
        self.rows, self.snps, self.width = rows, snps, width
        self.samp, self.snp = samp, snp
        self.total = COMPONENTS * width
        self.parts = 1
        for parts in (2, 4):
            span = snps // parts
            if span % LANES == 0 and width // (samp // min(samp, span // LANES)) >= 16:
                self.parts = parts
        self.span = snps // self.parts
        self.across = min(samp, self.span // LANES)
        self.down = samp // self.across
        self.high = width // self.down
        self.wide = self.span // self.across
        self.tile = min(rows, TILE_BYTES // (4 * self.span))
        self.tiles = rows // self.tile
        self.own = rows // snp
        self.chunk = min(128, self.own)
        self.chunks = self.own // self.chunk


def kernel(
    plan, geno, freq, bins, probes, variances, own, comb_rows,
    dosages, standard, acc, rs_send, rs_recv, gathered, counts, factor, weights,
    part_send, part_recv,
    in_sem, rs_ssem, rs_rsem, ag_ssem, ag_rsem, ct_ssem, ct_rsem, ex_ssem, ex_rsem,
):
    p = plan
    n, groups = p.samp, p.snp
    me, mine = lax.axis_index("samp"), lax.axis_index("snp")

    def fetch(step):
        part, tile, slot = step // p.tiles, step % p.tiles, step % DEPTH
        return pltpu.make_async_copy(
            geno.at[pl.ds(tile * p.tile, p.tile), pl.ds(pl.multiple_of(part * p.span, LANES), p.span)],
            dosages.at[slot],
            in_sem.at[slot],
        )

    steps = p.parts * p.tiles
    for step in range(min(DEPTH - 1, steps)):
        fetch(step).start()

    barrier = pltpu.get_barrier_semaphore()

    @pl.loop(1, n)
    def _(shift):
        pl.semaphore_signal(
            barrier, inc=1, device_id={"samp": (me + shift) % n, "snp": mine}, device_id_type=MESH
        )

    @pl.loop(1, groups)
    def _(shift):
        pl.semaphore_signal(
            barrier, inc=1, device_id={"samp": me, "snp": (mine + shift) % groups}, device_id_type=MESH
        )

    labels = lax.broadcasted_iota(jnp.int32, (LABELS, p.snps), 0)
    hits = labels == bins[...]
    counted = jnp.sum(hits.astype(F32), axis=1, keepdims=True)
    counts[0] = jnp.broadcast_to(counted, (LABELS, LANES))
    acc[...] = jnp.zeros_like(acc)
    pl.semaphore_wait(barrier, n - 1 + groups - 1)

    def count_copy(shift):
        return pltpu.make_async_remote_copy(
            src_ref=counts.at[0], dst_ref=counts.at[shift],
            send_sem=ct_ssem.at[shift - 1], recv_sem=ct_rsem.at[shift - 1],
            device_id={"samp": me, "snp": (mine + shift) % groups}, device_id_type=MESH,
        )

    for shift in range(1, groups):
        count_copy(shift).start()

    def scatter_copy(part, shift):
        peer = (me + shift) % n
        return pltpu.make_async_remote_copy(
            src_ref=rs_send.at[part, peer], dst_ref=rs_recv.at[part, shift - 1],
            send_sem=rs_ssem.at[part, shift - 1], recv_sem=rs_rsem.at[part, shift - 1],
            device_id={"samp": peer, "snp": mine}, device_id_type=MESH,
        )

    def gather_copy(part, shift):
        return pltpu.make_async_remote_copy(
            src_ref=gathered.at[part, me], dst_ref=gathered.at[part, me],
            send_sem=ag_ssem.at[part, shift - 1], recv_sem=ag_rsem.at[part, shift - 1],
            device_id={"samp": (me + shift) % n, "snp": mine}, device_id_type=MESH,
        )

    def arrival(part, shift):
        source = (me + n - shift) % n
        return pltpu.make_async_remote_copy(
            src_ref=gathered.at[part, source], dst_ref=gathered.at[part, source],
            send_sem=ag_ssem.at[part, shift - 1], recv_sem=ag_rsem.at[part, shift - 1],
            device_id={"samp": source, "snp": mine}, device_id_type=MESH,
        )

    def read_part(part):
        columns = slice(part * p.span, (part + 1) * p.span)
        allele = freq[:, columns]
        center = 2.0 * allele
        scale = 1.0 / jnp.sqrt(center * (1.0 - allele))

        @pl.loop(0, p.tiles)
        def _(tile):
            step = part * p.tiles + tile

            @pl.when(step + DEPTH - 1 < steps)
            def _():
                fetch(step + DEPTH - 1).start()

            fetch(step).wait()
            rows = pl.ds(pl.multiple_of(tile * p.tile, p.tile), p.tile)
            value = ((dosages[step % DEPTH].astype(F32) - center) * scale).astype(BF16)
            standard[rows, columns] = value
            acc[:, columns] += jnp.dot(probes[:, rows], value, preferred_element_type=F32)

        for piece in range(n):
            top, left = (piece // p.across) * p.high, part * p.span + (piece % p.across) * p.wide
            rs_send[part, piece] = acc[top : top + p.high, left : left + p.wide].astype(BF16)

        @pl.loop(1, n)
        def _(shift):
            scatter_copy(part, shift).start()

    def reduce_part(part):
        def add(shift, total):
            scatter_copy(part, shift).wait_recv()
            return total + rs_recv[part, shift - 1].astype(F32)

        total = lax.fori_loop(1, n, add, rs_send[part, me].astype(F32))
        left = pl.multiple_of(part * p.span + (me % p.across) * p.wide, LANES)
        whole_rows = jnp.float32(p.rows * n)
        scores = total / jnp.sqrt(whole_rows)
        gathered[part, me] = (scores * factor[0:1, pl.ds(left, p.wide)]).astype(BF16)

        @pl.loop(1, n)
        def _(shift):
            gather_copy(part, shift).start()

    def spread_part(part):
        @pl.loop(1, n)
        def _(shift):
            arrival(part, shift).wait_recv()

        repeat = LANES // p.width
        for column in range(p.across):
            left = part * p.span + column * p.wide
            pieces = [gathered[part, column + p.across * row].astype(F32) for row in range(p.down)]
            block = jnp.concatenate(pieces * repeat, axis=0)
            turned = block.T
            marks = jnp.broadcast_to(bins[:, left : left + p.wide].astype(F32), (LANES, p.wide)).T
            lane = lax.broadcasted_iota(jnp.int32, (p.wide, LANES), 1) // p.width
            for pair in range(p.total // LANES):
                label = (lane + pair * repeat).astype(F32)
                weights[left : left + p.wide, pair * LANES : (pair + 1) * LANES] = jnp.where(
                    marks == label, turned, 0.0
                ).astype(BF16)

    read_part(0)
    for shift in range(1, groups):
        count_copy(shift).wait_recv()
    whole = counts[0]
    for shift in range(1, groups):
        whole = whole + counts[shift]
    root = lax.rsqrt(whole[:, 0:1])
    row = jnp.sum(jnp.where(hits, root, 0.0), axis=0, keepdims=True)
    factor[...] = jnp.broadcast_to(row, factor.shape)
    for part in range(1, p.parts):
        read_part(part)
        if part >= 2:
            reduce_part(part - 2)
    for part in range(max(p.parts - 2, 0), p.parts):
        reduce_part(part)
    for part in range(p.parts):
        spread_part(part)

    def part_copy(index):
        shift, chunk = index // p.chunks, index % p.chunks
        rows = pl.ds(pl.multiple_of(chunk * p.chunk, p.chunk), p.chunk)
        return pltpu.make_async_remote_copy(
            src_ref=part_send.at[shift, rows], dst_ref=part_recv.at[shift, rows],
            send_sem=ex_ssem.at[index], recv_sem=ex_rsem.at[index],
            device_id={"samp": me, "snp": (mine + shift + 1) % groups}, device_id_type=MESH,
        )

    sends = (groups - 1) * p.chunks

    @pl.loop(0, sends)
    def _(index):
        shift, chunk = index // p.chunks, index % p.chunks
        target = (mine + shift + 1) % groups
        rows = pl.ds(pl.multiple_of(target * p.own + chunk * p.chunk, p.chunk), p.chunk)
        product = jnp.dot(standard[rows, :], weights[...], preferred_element_type=F32)
        part_send[shift, pl.ds(pl.multiple_of(chunk * p.chunk, p.chunk), p.chunk), :] = product.astype(BF16)
        part_copy(index).start()

    @pl.loop(0, p.chunks)
    def _(chunk):
        rows = pl.ds(pl.multiple_of(mine * p.own + chunk * p.chunk, p.chunk), p.chunk)
        here = pl.ds(pl.multiple_of(chunk * p.chunk, p.chunk), p.chunk)
        own[here, :] = jnp.dot(standard[rows, :], weights[...], preferred_element_type=F32)

    repeat = LANES // p.width
    lane = lax.broadcasted_iota(jnp.int32, (1, LANES), 1) // p.width
    lane_vars = []
    for pair in range(p.total // LANES):
        row = jnp.full((1, LANES), variances[pair * repeat], F32)
        for again in range(1, repeat):
            row = jnp.where(lane == again, variances[pair * repeat + again], row)
        lane_vars.append(row)
    noise = variances[COMPONENTS]

    @pl.loop(0, p.chunks)
    def _(chunk):
        here = pl.ds(pl.multiple_of(chunk * p.chunk, p.chunk), p.chunk)
        total = own[here, :]
        for shift in range(groups - 1):
            part_copy(shift * p.chunks + chunk).wait_recv()
            total = total + part_recv[shift, here, :].astype(F32)
        own[here, :] = total
        folded = jnp.zeros((p.chunk, LANES), F32)
        for pair in range(p.total // LANES):
            lanes = slice(pair * LANES, (pair + 1) * LANES)
            folded = folded + total[:, lanes] * lane_vars[pair]
        turned = folded.T
        mixed = turned[0 : p.width]
        for again in range(1, LANES // p.width):
            mixed = mixed + turned[again * p.width : (again + 1) * p.width]
        cols = pl.ds(pl.multiple_of(mine * p.own + chunk * p.chunk, p.chunk), p.chunk)
        comb_rows[:, here] = mixed + noise * probes[:, cols].astype(F32)

    @pl.loop(0, sends)
    def _(index):
        part_copy(index).wait_send()

    for part in range(p.parts):

        @pl.loop(1, n)
        def _(shift):
            scatter_copy(part, shift).wait_send()
            gather_copy(part, shift).wait_send()

    for shift in range(1, groups):
        count_copy(shift).wait_send()


def body(genotypes, allele_freq, snp_bins, probes, variances):
    rows, snps = genotypes.shape
    width = probes.shape[0]
    p = Plan(rows, snps, width, lax.axis_size("samp"), lax.axis_size("snp"))
    n, groups = p.samp, p.snp
    vmem, hbm = pl.BlockSpec(memory_space=pltpu.VMEM), pl.BlockSpec(memory_space=pl.ANY)
    dma = pltpu.SemaphoreType.DMA
    sends = (groups - 1) * p.chunks
    return pl.pallas_call(
        functools.partial(kernel, p),
        out_shape=(
            pltpu.VMEM((p.own, p.total), F32),
            pltpu.VMEM((width, p.own), F32),
        ),
        in_specs=[hbm, vmem, vmem, vmem, pl.BlockSpec(memory_space=pltpu.SMEM)],
        out_specs=(vmem, vmem),
        scratch_shapes=[
            pltpu.VMEM((DEPTH, p.tile, p.span), jnp.int32),
            pltpu.VMEM((rows, snps), BF16),
            pltpu.VMEM((width, snps), F32),
            pltpu.VMEM((p.parts, n, p.high, p.wide), BF16),
            pltpu.VMEM((p.parts, n - 1, p.high, p.wide), BF16),
            pltpu.VMEM((p.parts, n, p.high, p.wide), BF16),
            pltpu.VMEM((groups, LABELS, LANES), F32),
            pltpu.VMEM((8, snps), F32),
            pltpu.VMEM((snps, p.total), BF16),
            pltpu.VMEM((groups - 1, p.own, p.total), BF16),
            pltpu.VMEM((groups - 1, p.own, p.total), BF16),
            dma((DEPTH,)),
            dma((p.parts, n - 1)), dma((p.parts, n - 1)),
            dma((p.parts, n - 1)), dma((p.parts, n - 1)),
            dma((groups - 1,)), dma((groups - 1,)),
            dma((sends,)), dma((sends,)),
        ],
        compiler_params=pltpu.CompilerParams(
            collective_id=0, has_side_effects=True, vmem_limit_bytes=44 << 20
        ),
    )(genotypes, allele_freq[None, :], snp_bins[None, :], probes, variances)


def solution(mesh):
    placed = (P("samp", "snp"), P("snp"), P("snp"), P(None, "samp"), P())
    return jax.shard_map(
        body,
        mesh=mesh,
        in_specs=placed,
        out_specs=(P(("samp", "snp"), None), P(None, ("samp", "snp"))),
        check_vma=False,
    )
```

```python
import functools

import jax
import jax.numpy as jnp
from jax import lax
from jax.experimental import pallas as pl
from jax.experimental.pallas import tpu as pltpu
from jax.sharding import PartitionSpec as P

COMPONENTS = 12
LABELS = 16
LANES = 128
TILE_BYTES = 2 << 20
DEPTH = 8
VMEM_BYTES = 67_043_328
MESH = pl.DeviceIdType.MESH
F32 = jnp.float32
BF16 = jnp.bfloat16


class Plan:
    def __init__(self, rows, snps, width, samp, snp):
        self.rows, self.snps, self.width = rows, snps, width
        self.samp, self.snp = samp, snp
        self.total = COMPONENTS * width
        self.parts = 1
        for parts in (2, 4):
            span = snps // parts
            if span % LANES == 0 and width // (samp // min(samp, span // LANES)) >= 16:
                self.parts = parts
        self.span = snps // self.parts
        self.across = min(samp, self.span // LANES)
        self.down = samp // self.across
        self.high = width // self.down
        self.wide = self.span // self.across
        self.tile = min(rows, TILE_BYTES // (4 * self.span))
        self.tiles = rows // self.tile
        self.own = rows // snp
        self.chunk = min(128, self.own)
        self.chunks = self.own // self.chunk


def kernel(
    plan, geno, freq_in, bins_in, probes_in, variances, own, comb_rows,
    freq, bins, probes,
    dosages, standard, acc, rs_send, rs_recv, gathered, counts, factor, weights,
    part_send, part_recv,
    small_sem, in_sem, rs_ssem, rs_rsem, ag_ssem, ag_rsem, ct_ssem, ct_rsem, ex_ssem, ex_rsem,
):
    p = plan
    n, groups = p.samp, p.snp
    me, mine = lax.axis_index("samp"), lax.axis_index("snp")

    def fetch(step):
        part, tile, slot = step // p.tiles, step % p.tiles, step % DEPTH
        return pltpu.make_async_copy(
            geno.at[pl.ds(tile * p.tile, p.tile), pl.ds(pl.multiple_of(part * p.span, LANES), p.span)],
            dosages.at[slot],
            in_sem.at[slot],
        )

    small = [
        pltpu.make_async_copy(source, held, small_sem.at[place])
        for place, (source, held) in enumerate(((bins_in, bins), (freq_in, freq), (probes_in, probes)))
    ]
    for copy in small:
        copy.start()

    steps = p.parts * p.tiles
    for step in range(min(DEPTH - 1, steps)):
        fetch(step).start()

    barrier = pltpu.get_barrier_semaphore()

    @pl.loop(1, n)
    def _(shift):
        pl.semaphore_signal(
            barrier, inc=1, device_id={"samp": (me + shift) % n, "snp": mine}, device_id_type=MESH
        )

    @pl.loop(1, groups)
    def _(shift):
        pl.semaphore_signal(
            barrier, inc=1, device_id={"samp": me, "snp": (mine + shift) % groups}, device_id_type=MESH
        )

    for copy in small:
        copy.wait()
    labels = lax.broadcasted_iota(jnp.int32, (LABELS, p.snps), 0)
    hits = labels == bins[...]
    counted = jnp.sum(hits.astype(F32), axis=1, keepdims=True)
    counts[0] = jnp.broadcast_to(counted, (LABELS, LANES))
    acc[...] = jnp.zeros_like(acc)
    pl.semaphore_wait(barrier, n - 1 + groups - 1)

    def count_copy(shift):
        return pltpu.make_async_remote_copy(
            src_ref=counts.at[0], dst_ref=counts.at[shift],
            send_sem=ct_ssem.at[shift - 1], recv_sem=ct_rsem.at[shift - 1],
            device_id={"samp": me, "snp": (mine + shift) % groups}, device_id_type=MESH,
        )

    for shift in range(1, groups):
        count_copy(shift).start()

    def scatter_copy(part, shift):
        peer = (me + shift) % n
        return pltpu.make_async_remote_copy(
            src_ref=rs_send.at[part, peer], dst_ref=rs_recv.at[part, shift - 1],
            send_sem=rs_ssem.at[part, shift - 1], recv_sem=rs_rsem.at[part, shift - 1],
            device_id={"samp": peer, "snp": mine}, device_id_type=MESH,
        )

    def gather_copy(part, shift):
        return pltpu.make_async_remote_copy(
            src_ref=gathered.at[part, me], dst_ref=gathered.at[part, me],
            send_sem=ag_ssem.at[part, shift - 1], recv_sem=ag_rsem.at[part, shift - 1],
            device_id={"samp": (me + shift) % n, "snp": mine}, device_id_type=MESH,
        )

    def arrival(part, shift):
        source = (me + n - shift) % n
        return pltpu.make_async_remote_copy(
            src_ref=gathered.at[part, source], dst_ref=gathered.at[part, source],
            send_sem=ag_ssem.at[part, shift - 1], recv_sem=ag_rsem.at[part, shift - 1],
            device_id={"samp": source, "snp": mine}, device_id_type=MESH,
        )

    def read_part(part):
        columns = slice(part * p.span, (part + 1) * p.span)
        allele = freq[:, columns]
        center = 2.0 * allele
        scale = 1.0 / jnp.sqrt(center * (1.0 - allele))

        @pl.loop(0, p.tiles)
        def _(tile):
            step = part * p.tiles + tile

            @pl.when(step + DEPTH - 1 < steps)
            def _():
                fetch(step + DEPTH - 1).start()

            fetch(step).wait()
            rows = pl.ds(pl.multiple_of(tile * p.tile, p.tile), p.tile)
            value = ((dosages[step % DEPTH].astype(F32) - center) * scale).astype(BF16)
            standard[rows, columns] = value
            acc[:, columns] += jnp.dot(probes[:, rows], value, preferred_element_type=F32)

        for piece in range(n):
            top, left = (piece // p.across) * p.high, part * p.span + (piece % p.across) * p.wide
            rs_send[part, piece] = acc[top : top + p.high, left : left + p.wide].astype(BF16)

        @pl.loop(1, n)
        def _(shift):
            scatter_copy(part, shift).start()

    def reduce_part(part):
        def add(shift, total):
            scatter_copy(part, shift).wait_recv()
            return total + rs_recv[part, shift - 1].astype(F32)

        total = lax.fori_loop(1, n, add, rs_send[part, me].astype(F32))
        left = pl.multiple_of(part * p.span + (me % p.across) * p.wide, LANES)
        whole_rows = jnp.float32(p.rows * n)
        scores = total / jnp.sqrt(whole_rows)
        gathered[part, me] = (scores * factor[0:1, pl.ds(left, p.wide)]).astype(BF16)

        @pl.loop(1, n)
        def _(shift):
            gather_copy(part, shift).start()

    def spread_part(part):
        @pl.loop(1, n)
        def _(shift):
            arrival(part, shift).wait_recv()

        repeat = LANES // p.width
        for column in range(p.across):
            left = part * p.span + column * p.wide
            pieces = [gathered[part, column + p.across * row].astype(F32) for row in range(p.down)]
            block = jnp.concatenate(pieces * repeat, axis=0)
            turned = block.T
            marks = jnp.broadcast_to(bins[:, left : left + p.wide].astype(F32), (LANES, p.wide)).T
            lane = lax.broadcasted_iota(jnp.int32, (p.wide, LANES), 1) // p.width
            for pair in range(p.total // LANES):
                label = (lane + pair * repeat).astype(F32)
                weights[left : left + p.wide, pair * LANES : (pair + 1) * LANES] = jnp.where(
                    marks == label, turned, 0.0
                ).astype(BF16)

    read_part(0)
    for shift in range(1, groups):
        count_copy(shift).wait_recv()
    whole = counts[0]
    for shift in range(1, groups):
        whole = whole + counts[shift]
    root = lax.rsqrt(whole[:, 0:1])
    row = jnp.sum(jnp.where(hits, root, 0.0), axis=0, keepdims=True)
    factor[...] = jnp.broadcast_to(row, factor.shape)
    for part in range(1, p.parts):
        read_part(part)
        if part >= 2:
            reduce_part(part - 2)
    for part in range(max(p.parts - 2, 0), p.parts):
        reduce_part(part)
    for part in range(p.parts):
        spread_part(part)

    def part_copy(index):
        shift, chunk = index // p.chunks, index % p.chunks
        rows = pl.ds(pl.multiple_of(chunk * p.chunk, p.chunk), p.chunk)
        return pltpu.make_async_remote_copy(
            src_ref=part_send.at[shift, rows], dst_ref=part_recv.at[shift, rows],
            send_sem=ex_ssem.at[index], recv_sem=ex_rsem.at[index],
            device_id={"samp": me, "snp": (mine + shift + 1) % groups}, device_id_type=MESH,
        )

    sends = (groups - 1) * p.chunks

    @pl.loop(0, sends)
    def _(index):
        shift, chunk = index // p.chunks, index % p.chunks
        target = (mine + shift + 1) % groups
        rows = pl.ds(pl.multiple_of(target * p.own + chunk * p.chunk, p.chunk), p.chunk)
        product = jnp.dot(standard[rows, :], weights[...], preferred_element_type=F32)
        part_send[shift, pl.ds(pl.multiple_of(chunk * p.chunk, p.chunk), p.chunk), :] = product.astype(BF16)
        part_copy(index).start()

    @pl.loop(0, p.chunks)
    def _(chunk):
        rows = pl.ds(pl.multiple_of(mine * p.own + chunk * p.chunk, p.chunk), p.chunk)
        here = pl.ds(pl.multiple_of(chunk * p.chunk, p.chunk), p.chunk)
        own[here, :] = jnp.dot(standard[rows, :], weights[...], preferred_element_type=F32)

    repeat = LANES // p.width
    lane = lax.broadcasted_iota(jnp.int32, (1, LANES), 1) // p.width
    lane_vars = []
    for pair in range(p.total // LANES):
        row = jnp.full((1, LANES), variances[pair * repeat], F32)
        for again in range(1, repeat):
            row = jnp.where(lane == again, variances[pair * repeat + again], row)
        lane_vars.append(row)
    noise = variances[COMPONENTS]

    @pl.loop(0, p.chunks)
    def _(chunk):
        here = pl.ds(pl.multiple_of(chunk * p.chunk, p.chunk), p.chunk)
        total = own[here, :]
        for shift in range(groups - 1):
            part_copy(shift * p.chunks + chunk).wait_recv()
            total = total + part_recv[shift, here, :].astype(F32)
        own[here, :] = total
        folded = jnp.zeros((p.chunk, LANES), F32)
        for pair in range(p.total // LANES):
            lanes = slice(pair * LANES, (pair + 1) * LANES)
            folded = folded + total[:, lanes] * lane_vars[pair]
        turned = folded.T
        mixed = turned[0 : p.width]
        for again in range(1, LANES // p.width):
            mixed = mixed + turned[again * p.width : (again + 1) * p.width]
        cols = pl.ds(pl.multiple_of(mine * p.own + chunk * p.chunk, p.chunk), p.chunk)
        comb_rows[:, here] = mixed + noise * probes[:, cols].astype(F32)

    @pl.loop(0, sends)
    def _(index):
        part_copy(index).wait_send()

    for part in range(p.parts):

        @pl.loop(1, n)
        def _(shift):
            scatter_copy(part, shift).wait_send()
            gather_copy(part, shift).wait_send()

    for shift in range(1, groups):
        count_copy(shift).wait_send()


def body(genotypes, allele_freq, snp_bins, probes, variances):
    rows, snps = genotypes.shape
    width = probes.shape[0]
    p = Plan(rows, snps, width, lax.axis_size("samp"), lax.axis_size("snp"))
    n, groups = p.samp, p.snp
    vmem, hbm = pl.BlockSpec(memory_space=pltpu.VMEM), pl.BlockSpec(memory_space=pl.ANY)
    held = pl.BlockSpec(memory_space=pltpu.HBM)
    dma = pltpu.SemaphoreType.DMA
    sends = (groups - 1) * p.chunks
    return pl.pallas_call(
        functools.partial(kernel, p),
        out_shape=(
            pltpu.VMEM((p.own, p.total), F32),
            pltpu.VMEM((width, p.own), F32),
        ),
        in_specs=[hbm, held, held, held, pl.BlockSpec(memory_space=pltpu.SMEM)],
        out_specs=(vmem, vmem),
        scratch_shapes=[
            pltpu.VMEM((1, snps), F32),
            pltpu.VMEM((1, snps), jnp.int32),
            pltpu.VMEM((width, rows), BF16),
            pltpu.VMEM((DEPTH, p.tile, p.span), jnp.int32),
            pltpu.VMEM((rows, snps), BF16),
            pltpu.VMEM((width, snps), F32),
            pltpu.VMEM((p.parts, n, p.high, p.wide), BF16),
            pltpu.VMEM((p.parts, n - 1, p.high, p.wide), BF16),
            pltpu.VMEM((p.parts, n, p.high, p.wide), BF16),
            pltpu.VMEM((groups, LABELS, LANES), F32),
            pltpu.VMEM((8, snps), F32),
            pltpu.VMEM((snps, p.total), BF16),
            pltpu.VMEM((groups - 1, p.own, p.total), BF16),
            pltpu.VMEM((groups - 1, p.own, p.total), BF16),
            dma((3,)),
            dma((DEPTH,)),
            dma((p.parts, n - 1)), dma((p.parts, n - 1)),
            dma((p.parts, n - 1)), dma((p.parts, n - 1)),
            dma((groups - 1,)), dma((groups - 1,)),
            dma((sends,)), dma((sends,)),
        ],
        compiler_params=pltpu.CompilerParams(
            collective_id=0, has_side_effects=True, vmem_limit_bytes=VMEM_BYTES - 4 * p.own * (p.total + width) - 8192
        ),
    )(genotypes, allele_freq[None, :], snp_bins[None, :], probes, variances)


def solution(mesh):
    placed = (P("samp", "snp"), P("snp"), P("snp"), P(None, "samp"), P())
    return jax.shard_map(
        body,
        mesh=mesh,
        in_specs=placed,
        out_specs=(P(("samp", "snp"), None), P(None, ("samp", "snp"))),
        check_vma=False,
    )
```

```python
import functools

import jax
import jax.numpy as jnp
from jax import lax
from jax.experimental import pallas as pl
from jax.experimental.pallas import tpu as pltpu
from jax.sharding import PartitionSpec as P

COMPONENTS = 12
LABELS = 16
LANES = 128
TILE_BYTES = 4 << 20
DEPTH = 5
VMEM_BYTES = 67_043_328
MESH = pl.DeviceIdType.MESH
F32 = jnp.float32
BF16 = jnp.bfloat16


class Plan:
    def __init__(self, rows, snps, width, samp, snp):
        self.rows, self.snps, self.width = rows, snps, width
        self.samp, self.snp = samp, snp
        self.total = COMPONENTS * width
        self.parts = 1
        for parts in (2, 4):
            span = snps // parts
            if span % LANES == 0 and width // (samp // min(samp, span // LANES)) >= 16:
                self.parts = parts
        self.span = snps // self.parts
        self.across = min(samp, self.span // LANES)
        self.down = samp // self.across
        self.high = width // self.down
        self.wide = self.span // self.across
        self.tile = min(rows, TILE_BYTES // (4 * self.span))
        self.tiles = rows // self.tile
        self.own = rows // snp
        self.chunk = min(128, self.own)
        self.chunks = self.own // self.chunk


def kernel(
    plan, geno, freq_in, bins_in, probes_in, variances, own, comb_rows,
    freq, bins, probes,
    dosages, standard, acc, rs_send, rs_recv, gathered, counts, factor, weights,
    part_send, part_recv,
    small_sem, in_sem, rs_ssem, rs_rsem, ag_ssem, ag_rsem, ct_ssem, ct_rsem, ex_ssem, ex_rsem,
):
    p = plan
    n, groups = p.samp, p.snp
    me, mine = lax.axis_index("samp"), lax.axis_index("snp")

    def fetch(step):
        part, tile, slot = step // p.tiles, step % p.tiles, step % DEPTH
        return pltpu.make_async_copy(
            geno.at[pl.ds(tile * p.tile, p.tile), pl.ds(pl.multiple_of(part * p.span, LANES), p.span)],
            dosages.at[slot],
            in_sem.at[slot],
        )

    small = [
        pltpu.make_async_copy(source, held, small_sem.at[place])
        for place, (source, held) in enumerate(((bins_in, bins), (freq_in, freq), (probes_in, probes)))
    ]
    for copy in small:
        copy.start()

    steps = p.parts * p.tiles
    for step in range(min(DEPTH - 1, steps)):
        fetch(step).start()

    barrier = pltpu.get_barrier_semaphore()

    @pl.loop(1, n)
    def _(shift):
        pl.semaphore_signal(
            barrier, inc=1, device_id={"samp": (me + shift) % n, "snp": mine}, device_id_type=MESH
        )

    @pl.loop(1, groups)
    def _(shift):
        pl.semaphore_signal(
            barrier, inc=1, device_id={"samp": me, "snp": (mine + shift) % groups}, device_id_type=MESH
        )

    for copy in small:
        copy.wait()
    labels = lax.broadcasted_iota(jnp.int32, (LABELS, p.snps), 0)
    hits = labels == bins[...]
    counted = jnp.sum(hits.astype(F32), axis=1, keepdims=True)
    counts[0] = jnp.broadcast_to(counted, (LABELS, LANES))
    acc[...] = jnp.zeros_like(acc)
    pl.semaphore_wait(barrier, n - 1 + groups - 1)

    def count_copy(shift):
        return pltpu.make_async_remote_copy(
            src_ref=counts.at[0], dst_ref=counts.at[shift],
            send_sem=ct_ssem.at[shift - 1], recv_sem=ct_rsem.at[shift - 1],
            device_id={"samp": me, "snp": (mine + shift) % groups}, device_id_type=MESH,
        )

    for shift in range(1, groups):
        count_copy(shift).start()

    def scatter_copy(part, shift):
        peer = (me + shift) % n
        return pltpu.make_async_remote_copy(
            src_ref=rs_send.at[part, peer], dst_ref=rs_recv.at[part, shift - 1],
            send_sem=rs_ssem.at[part, shift - 1], recv_sem=rs_rsem.at[part, shift - 1],
            device_id={"samp": peer, "snp": mine}, device_id_type=MESH,
        )

    def gather_copy(part, shift):
        return pltpu.make_async_remote_copy(
            src_ref=gathered.at[part, me], dst_ref=gathered.at[part, me],
            send_sem=ag_ssem.at[part, shift - 1], recv_sem=ag_rsem.at[part, shift - 1],
            device_id={"samp": (me + shift) % n, "snp": mine}, device_id_type=MESH,
        )

    def arrival(part, shift):
        source = (me + n - shift) % n
        return pltpu.make_async_remote_copy(
            src_ref=gathered.at[part, source], dst_ref=gathered.at[part, source],
            send_sem=ag_ssem.at[part, shift - 1], recv_sem=ag_rsem.at[part, shift - 1],
            device_id={"samp": source, "snp": mine}, device_id_type=MESH,
        )

    def read_part(part):
        columns = slice(part * p.span, (part + 1) * p.span)
        allele = freq[:, columns]
        center = 2.0 * allele
        scale = 1.0 / jnp.sqrt(center * (1.0 - allele))

        @pl.loop(0, p.tiles)
        def _(tile):
            step = part * p.tiles + tile

            @pl.when(step + DEPTH - 1 < steps)
            def _():
                fetch(step + DEPTH - 1).start()

            fetch(step).wait()
            rows = pl.ds(pl.multiple_of(tile * p.tile, p.tile), p.tile)
            value = ((dosages[step % DEPTH].astype(F32) - center) * scale).astype(BF16)
            standard[rows, columns] = value
            acc[:, columns] += jnp.dot(probes[:, rows], value, preferred_element_type=F32)

        for piece in range(n):
            top, left = (piece // p.across) * p.high, part * p.span + (piece % p.across) * p.wide
            rs_send[part, piece] = acc[top : top + p.high, left : left + p.wide].astype(BF16)

        @pl.loop(1, n)
        def _(shift):
            scatter_copy(part, shift).start()

    def reduce_part(part):
        def add(shift, total):
            scatter_copy(part, shift).wait_recv()
            return total + rs_recv[part, shift - 1].astype(F32)

        total = lax.fori_loop(1, n, add, rs_send[part, me].astype(F32))
        left = pl.multiple_of(part * p.span + (me % p.across) * p.wide, LANES)
        whole_rows = jnp.float32(p.rows * n)
        scores = total / jnp.sqrt(whole_rows)
        gathered[part, me] = (scores * factor[0:1, pl.ds(left, p.wide)]).astype(BF16)

        @pl.loop(1, n)
        def _(shift):
            gather_copy(part, shift).start()

    def spread_part(part):
        @pl.loop(1, n)
        def _(shift):
            arrival(part, shift).wait_recv()

        repeat = LANES // p.width
        for column in range(p.across):
            left = part * p.span + column * p.wide
            pieces = [gathered[part, column + p.across * row].astype(F32) for row in range(p.down)]
            block = jnp.concatenate(pieces * repeat, axis=0)
            turned = block.T
            marks = jnp.broadcast_to(bins[:, left : left + p.wide].astype(F32), (LANES, p.wide)).T
            lane = lax.broadcasted_iota(jnp.int32, (p.wide, LANES), 1) // p.width
            for pair in range(p.total // LANES):
                label = (lane + pair * repeat).astype(F32)
                weights[left : left + p.wide, pair * LANES : (pair + 1) * LANES] = jnp.where(
                    marks == label, turned, 0.0
                ).astype(BF16)

    read_part(0)
    for shift in range(1, groups):
        count_copy(shift).wait_recv()
    whole = counts[0]
    for shift in range(1, groups):
        whole = whole + counts[shift]
    root = lax.rsqrt(whole[:, 0:1])
    row = jnp.sum(jnp.where(hits, root, 0.0), axis=0, keepdims=True)
    factor[...] = jnp.broadcast_to(row, factor.shape)
    for part in range(1, p.parts):
        read_part(part)
        if part >= 2:
            reduce_part(part - 2)
    early = max(p.parts - 2, 0)
    for part in range(early, p.parts - 1):
        reduce_part(part)
    for part in range(early):
        spread_part(part)
    reduce_part(p.parts - 1)
    for part in range(early, p.parts):
        spread_part(part)

    def part_copy(index):
        shift, chunk = index // p.chunks, index % p.chunks
        rows = pl.ds(pl.multiple_of(chunk * p.chunk, p.chunk), p.chunk)
        return pltpu.make_async_remote_copy(
            src_ref=part_send.at[shift, rows], dst_ref=part_recv.at[shift, rows],
            send_sem=ex_ssem.at[index], recv_sem=ex_rsem.at[index],
            device_id={"samp": me, "snp": (mine + shift + 1) % groups}, device_id_type=MESH,
        )

    sends = (groups - 1) * p.chunks

    @pl.loop(0, sends)
    def _(index):
        shift, chunk = index // p.chunks, index % p.chunks
        target = (mine + shift + 1) % groups
        rows = pl.ds(pl.multiple_of(target * p.own + chunk * p.chunk, p.chunk), p.chunk)
        product = jnp.dot(standard[rows, :], weights[...], preferred_element_type=F32)
        part_send[shift, pl.ds(pl.multiple_of(chunk * p.chunk, p.chunk), p.chunk), :] = product.astype(BF16)
        part_copy(index).start()

    @pl.loop(0, p.chunks)
    def _(chunk):
        rows = pl.ds(pl.multiple_of(mine * p.own + chunk * p.chunk, p.chunk), p.chunk)
        here = pl.ds(pl.multiple_of(chunk * p.chunk, p.chunk), p.chunk)
        own[here, :] = jnp.dot(standard[rows, :], weights[...], preferred_element_type=F32)

    repeat = LANES // p.width
    lane = lax.broadcasted_iota(jnp.int32, (1, LANES), 1) // p.width
    lane_vars = []
    for pair in range(p.total // LANES):
        row = jnp.full((1, LANES), variances[pair * repeat], F32)
        for again in range(1, repeat):
            row = jnp.where(lane == again, variances[pair * repeat + again], row)
        lane_vars.append(row)
    noise = variances[COMPONENTS]

    @pl.loop(0, p.chunks)
    def _(chunk):
        here = pl.ds(pl.multiple_of(chunk * p.chunk, p.chunk), p.chunk)
        total = own[here, :]
        for shift in range(groups - 1):
            part_copy(shift * p.chunks + chunk).wait_recv()
            total = total + part_recv[shift, here, :].astype(F32)
        own[here, :] = total
        folded = jnp.zeros((p.chunk, LANES), F32)
        for pair in range(p.total // LANES):
            lanes = slice(pair * LANES, (pair + 1) * LANES)
            folded = folded + total[:, lanes] * lane_vars[pair]
        turned = folded.T
        mixed = turned[0 : p.width]
        for again in range(1, LANES // p.width):
            mixed = mixed + turned[again * p.width : (again + 1) * p.width]
        cols = pl.ds(pl.multiple_of(mine * p.own + chunk * p.chunk, p.chunk), p.chunk)
        comb_rows[:, here] = mixed + noise * probes[:, cols].astype(F32)

    @pl.loop(0, sends)
    def _(index):
        part_copy(index).wait_send()

    for part in range(p.parts):

        @pl.loop(1, n)
        def _(shift):
            scatter_copy(part, shift).wait_send()
            gather_copy(part, shift).wait_send()

    for shift in range(1, groups):
        count_copy(shift).wait_send()


def body(genotypes, allele_freq, snp_bins, probes, variances):
    rows, snps = genotypes.shape
    width = probes.shape[0]
    p = Plan(rows, snps, width, lax.axis_size("samp"), lax.axis_size("snp"))
    n, groups = p.samp, p.snp
    vmem, hbm = pl.BlockSpec(memory_space=pltpu.VMEM), pl.BlockSpec(memory_space=pl.ANY)
    held = pl.BlockSpec(memory_space=pltpu.HBM)
    dma = pltpu.SemaphoreType.DMA
    sends = (groups - 1) * p.chunks
    return pl.pallas_call(
        functools.partial(kernel, p),
        out_shape=(
            pltpu.VMEM((p.own, p.total), F32),
            pltpu.VMEM((width, p.own), F32),
        ),
        in_specs=[hbm, held, held, held, pl.BlockSpec(memory_space=pltpu.SMEM)],
        out_specs=(vmem, vmem),
        scratch_shapes=[
            pltpu.VMEM((1, snps), F32),
            pltpu.VMEM((1, snps), jnp.int32),
            pltpu.VMEM((width, rows), BF16),
            pltpu.VMEM((DEPTH, p.tile, p.span), jnp.int32),
            pltpu.VMEM((rows, snps), BF16),
            pltpu.VMEM((width, snps), F32),
            pltpu.VMEM((p.parts, n, p.high, p.wide), BF16),
            pltpu.VMEM((p.parts, n - 1, p.high, p.wide), BF16),
            pltpu.VMEM((p.parts, n, p.high, p.wide), BF16),
            pltpu.VMEM((groups, LABELS, LANES), F32),
            pltpu.VMEM((8, snps), F32),
            pltpu.VMEM((snps, p.total), BF16),
            pltpu.VMEM((groups - 1, p.own, p.total), BF16),
            pltpu.VMEM((groups - 1, p.own, p.total), BF16),
            dma((3,)),
            dma((DEPTH,)),
            dma((p.parts, n - 1)), dma((p.parts, n - 1)),
            dma((p.parts, n - 1)), dma((p.parts, n - 1)),
            dma((groups - 1,)), dma((groups - 1,)),
            dma((sends,)), dma((sends,)),
        ],
        compiler_params=pltpu.CompilerParams(
            collective_id=0, has_side_effects=True, vmem_limit_bytes=VMEM_BYTES - 4 * p.own * (p.total + width) - 8192
        ),
    )(genotypes, allele_freq[None, :], snp_bins[None, :], probes, variances)


def solution(mesh):
    placed = (P("samp", "snp"), P("snp"), P("snp"), P(None, "samp"), P())
    return jax.shard_map(
        body,
        mesh=mesh,
        in_specs=placed,
        out_specs=(P(("samp", "snp"), None), P(None, ("samp", "snp"))),
        check_vma=False,
    )
```
